32 devices in a mesh: groups: 2 (over y), expert: 4 (over z), dp: 4 (over x, core).
Axes of the slice: x: 2, y: 2, z: 4, core: 2. Of those that a mesh axis runs over, the one named last changes fastest.
Arguments:
- tokens: bfloat16 [4096, 1280], P(('groups', 'expert', 'dp')), parts along dimension 0, may hold values from -6 to 6
- cotangent: bfloat16 [4096, 1280], P(('groups', 'expert', 'dp')), parts along dimension 0, may hold values from -3 to 3
- expert_ids: int32 [4096, 6], P(('groups', 'expert', 'dp')), parts along dimension 0, may hold values from 0 to 15, all different within a row; in each aligned block of 128 rows (0 to 127, 128 to 255, ...) at most 52 rows name the same one
- gate_values: bfloat16 [4096, 6], P(('groups', 'expert', 'dp')), parts along dimension 0, may hold values from 0.099609375 to 1
- gate_weight: bfloat16 [16, 1280, 768], P('expert'), may hold values from -0.15625 to 0.15625
- up_weight: bfloat16 [16, 1280, 768], P('expert'), may hold values from -0.15625 to 0.15625
- down_weight: bfloat16 [16, 768, 1280], P('expert'), may hold values from -0.21875 to 0.21875
Outputs:
- layer_out: bfloat16 [4096, 1280], P(('groups', 'expert', 'dp')), parts along dimension 0
- grad_tokens: bfloat16 [4096, 1280], P(('groups', 'expert', 'dp')), parts along dimension 0
- grad_gate: float32 [32, 1280, 768], P(('groups', 'expert'), 'dp'), parts along dimension 0
- grad_up: float32 [32, 1280, 768], P(('groups', 'expert'), 'dp'), parts along dimension 0
- grad_down: float32 [32, 768, 1280], P(('groups', 'expert'), 'dp'), parts along dimension 0
The draws below stay inside these ranges and needn't reach their ends.
There are 2 independent parts, one for each index of `groups`. The reference program is written for one: setup_inputs(seed, part) draws one part's arguments, and reference() takes and returns one part's arrays. A program takes and returns all parts, laid end to end along the dimension named above; an argument that names none is the same for every part. Nothing has to cross between parts.
Inputs may be any that keep to these rules, and one draw needn't show every extreme that they name: `expert_ids`: each row names 6 different experts. Among the 128 rows of one device (aligned blocks of rows), no expert is named by more than 52 rows, and in some blocks an expert is named by exactly 52 rows.
All inputs are finite; a program needn't handle non-finite values.
Results may differ from the reference program's by a relative error of at most 0.015.
Values may be sent and summed in bfloat16 or wider, within the bound.
A program may use at most 128 MiB of HBM per device.

```python
import math
import jax
import jax.numpy as jnp
import numpy as np
from jax import lax

D = 1280
FF = 768
TOPK = 6
TOK_DEV = 128
EXPERTS = 16
CAP = 52
TOKENS = 2048
N_EXPERT = 4
N_DP = 4


def steps_of(rng, dims, cuts, smallest, high):
    factor_of, own = 1.0, jax.random.fold_in(rng, 6)
    for axis_at, blocks in cuts:
        steps = jnp.exp(jax.random.uniform(jax.random.fold_in(own, axis_at), (blocks,), jnp.float32, smallest / len(cuts), high / len(cuts)))
        factor_of = factor_of * jnp.repeat(steps, dims[axis_at] // blocks).reshape([-1 if axis == axis_at else 1 for axis in range(len(dims))])
    return factor_of


def deal_out(key, own, number, rows, count, top, limit, skew):
    sequence = jax.random.permutation(key, count)
    packed, ordinary = portions_of(count, rows * top, limit, skew, True), portions_of(count, rows * top, limit, skew, False)
    places = jnp.arange(count)

    def named(lengths, offset_by):
        used = int((lengths > 0).sum())
        fixed = max(1, used // 4)
        moved = fixed + (places - fixed + offset_by * (used - fixed)) % max(1, count - fixed)
        return jnp.zeros((count,), jnp.int32).at[sequence[jnp.where(places < fixed, places, moved)]].set(jnp.asarray(lengths, jnp.int32))

    lengths = jnp.where(number % 4 == 0, named(packed, number // 4), named(ordinary, number - number // 4 - 1))
    mixed = jax.random.permutation(jax.random.fold_in(own, 3), count)
    source_of, sink = mixed[0:count // 2 * 2:2], mixed[1:count // 2 * 2:2]
    slack = jnp.minimum(lengths[source_of] - 1, limit - lengths[sink]) // 2
    slack = jnp.where((source_of == sequence[0]) | (sink == sequence[0]) | (lengths[sink] == 0), 0, jnp.maximum(slack, 0))
    moved = jax.random.randint(jax.random.fold_in(own, 4), (count // 2,), 0, 1 << 20) % (slack + 1)
    lengths = lengths.at[source_of].add(-moved).at[sink].add(moved)
    items = jnp.searchsorted(jnp.cumsum(lengths), jnp.arange(rows * top), side="right").astype(jnp.int32)
    grid = items.reshape(top, rows).T
    grid = grid[jax.random.permutation(jax.random.fold_in(own, 1), rows)]
    offset_by = jax.random.randint(jax.random.fold_in(own, 2), (rows, 1), 0, top)
    return jnp.take_along_axis(grid, (jnp.arange(top)[None, :] + offset_by) % top, axis=1)


def portions_of(number_of, total, bound, skew, full):
    loads = [(1 << 20) // math.isqrt(grade ** skew) + 1 for grade in range(1, number_of + 1)]
    largest = bound if full else min(bound, max(-(-total // number_of), total * loads[0] // sum(loads)))
    least = 1 if total - largest >= number_of - 1 else 0
    counts, spare = [largest] + [least] * (number_of - 1), total - largest - least * (number_of - 1)
    while spare > 0:
        candidates = [i for i in range(1, number_of) if counts[i] < largest] or [i for i in range(1, number_of) if counts[i] < bound]
        mass, remaining = sum([loads[i] for i in candidates]), spare
        for i in candidates:
            extra = min(bound - counts[i], max(1, remaining * loads[i] // mass), spare)
            counts[i] = counts[i] + extra
            spare = spare - extra
    return np.array(counts)


def bell_draw(rng, extent, scale, reach, split=(), kind=jnp.bfloat16):
    level = steps_of(rng, extent, split, -0.22, 0.18) if split else 1.0
    values = jax.random.normal(rng, extent, jnp.float32) * scale * level
    return jnp.minimum(jnp.maximum(values, -reach), reach).astype(kind)


def setup_inputs(seed: int = 0, part: int = 0) -> dict:
    seeds = jax.random.split(jax.random.key(seed), 8)
    part_splits = jax.random.split(jax.random.fold_in(seeds[7], part), 8)
    tokens = bell_draw(part_splits[0], (TOKENS, D), 1.0, 6.0, ((0, 16),))
    cotangent = bell_draw(part_splits[1], (TOKENS, D), 0.5, 3.0, ((0, 16),))
    expert_ids_keys = jax.random.split(jax.random.fold_in(part_splits[2], 1), TOKENS // TOK_DEV)
    expert_ids_turns = jax.random.permutation(jax.random.fold_in(part_splits[2], 3), TOKENS // TOK_DEV)
    expert_ids = jax.vmap(lambda own, number: deal_out(jax.random.fold_in(part_splits[2], 2), own, number, TOK_DEV, EXPERTS, TOPK, CAP, 1))(expert_ids_keys, expert_ids_turns).reshape((TOKENS, TOPK))
    gate_values = jnp.clip(0.099609375 + 0.9003906 * jax.random.uniform(part_splits[3], (TOKENS, TOPK), jnp.float32) ** steps_of(part_splits[3], (TOKENS, TOPK), ((0, 16),), -0.2, 0.2), 0.099609375, 1.0).astype(jnp.bfloat16)
    gate_weight = bell_draw(seeds[4], (EXPERTS, D, FF), D ** -0.5, 0.15625, ((0, 4),))
    up_weight = bell_draw(seeds[5], (EXPERTS, D, FF), D ** -0.5, 0.15625, ((0, 4),))
    down_weight = bell_draw(seeds[6], (EXPERTS, FF, D), FF ** -0.5, 0.21875, ((0, 4),))
    return dict(tokens=tokens, cotangent=cotangent, expert_ids=expert_ids, gate_values=gate_values, gate_weight=gate_weight, up_weight=up_weight, down_weight=down_weight)


def rounded(values):
    return lax.optimization_barrier(values.astype(jnp.bfloat16)).astype(jnp.float32)


def by_replica(values):
    shaped = values.reshape((N_EXPERT, N_DP, TOK_DEV) + values.shape[1:])
    shaped = jnp.swapaxes(shaped, 0, 1)
    return shaped.reshape((N_DP, N_EXPERT * TOK_DEV) + values.shape[1:])


def to_tokens(values):
    shaped = values.reshape(N_DP, N_EXPERT, TOK_DEV, D)
    return jnp.swapaxes(shaped, 0, 1).reshape(TOKENS, D)


def pick_rows(table, slot_rows):
    return jax.vmap(lambda matrix, index: jnp.take(matrix, index, axis=0))(table, slot_rows)


def reference(tokens, cotangent, expert_ids, gate_values, gate_weight, up_weight, down_weight):
    group_rows = N_EXPERT * TOK_DEV
    slot_count = group_rows * TOPK
    queue_rows = N_EXPERT * CAP
    token_rep = by_replica(tokens).astype(jnp.float32)
    grad_rep = by_replica(cotangent).astype(jnp.float32)
    ids_rep = by_replica(expert_ids).reshape(N_DP, slot_count)
    gates_rep = by_replica(gate_values).astype(jnp.float32).reshape(N_DP, slot_count)
    slot_token = jnp.broadcast_to((jnp.arange(slot_count, dtype=jnp.int32) // TOPK)[None, :], (N_DP, slot_count))
    replica = jnp.broadcast_to(jnp.arange(N_DP, dtype=jnp.int32)[:, None], (N_DP, slot_count))
    replica_rows = jnp.arange(N_DP, dtype=jnp.int32)[:, None]

    def per_expert(running, expert):
        out_sum, grad_sum = running
        chosen = ids_rep == expert
        slot_order = jnp.cumsum(chosen.astype(jnp.int32), axis=1).astype(jnp.int32) - 1
        slot_place = jnp.where(chosen, slot_order, queue_rows).astype(jnp.int32)
        slot_rows = jnp.zeros((N_DP, queue_rows + 1), jnp.int32).at[replica, slot_place].set(slot_token)[:, :queue_rows]
        weights = jnp.zeros((N_DP, queue_rows + 1), jnp.float32).at[replica, slot_place].set(gates_rep)[:, :queue_rows]
        gate_matrix = gate_weight[expert].astype(jnp.float32)
        up_matrix = up_weight[expert].astype(jnp.float32)
        down_matrix = down_weight[expert].astype(jnp.float32)
        inputs = pick_rows(token_rep, slot_rows)
        gate_sums = jnp.einsum("rqd,df->rqf", inputs, gate_matrix)
        up_sums = jnp.einsum("rqd,df->rqf", inputs, up_matrix)
        hidden = rounded(jax.nn.silu(gate_sums) * up_sums)
        expert_out = rounded(jnp.einsum("rqf,fd->rqd", hidden, down_matrix))
        out_sum = out_sum.at[replica_rows, slot_rows].add(weights[:, :, None] * expert_out)
        out_grad = rounded(weights[:, :, None] * pick_rows(grad_rep, slot_rows))
        hidden_grad = jnp.einsum("rqd,fd->rqf", out_grad, down_matrix)
        sigmoid = jax.nn.sigmoid(gate_sums)
        gate_back = rounded(hidden_grad * up_sums * sigmoid * (1.0 + gate_sums * (1.0 - sigmoid)))
        up_back = rounded(hidden_grad * (gate_sums * sigmoid))
        slot_grad = rounded(jnp.einsum("rqf,df->rqd", gate_back, gate_matrix) + jnp.einsum("rqf,df->rqd", up_back, up_matrix))
        grad_sum = grad_sum.at[replica_rows, slot_rows].add(slot_grad)
        part_gate = rounded(jnp.einsum("rqd,rqf->rdf", inputs, gate_back))
        part_up = rounded(jnp.einsum("rqd,rqf->rdf", inputs, up_back))
        part_down = rounded(jnp.einsum("rqf,rqd->rfd", hidden, out_grad))
        return (out_sum, grad_sum), (jnp.sum(part_gate, axis=0), jnp.sum(part_up, axis=0), jnp.sum(part_down, axis=0))

    start = (jnp.zeros((N_DP, group_rows, D), jnp.float32), jnp.zeros((N_DP, group_rows, D), jnp.float32))
    finals, stacked = lax.scan(per_expert, start, jnp.arange(EXPERTS, dtype=jnp.int32))
    out_sum, grad_sum = finals
    grad_gate, grad_up, grad_down = stacked
    return (to_tokens(out_sum).astype(jnp.bfloat16), to_tokens(grad_sum).astype(jnp.bfloat16), grad_gate, grad_up, grad_down)
```

```python
import functools

import jax
import jax.numpy as jnp
from jax import lax
from jax.experimental import pallas as pl
from jax.experimental.pallas import tpu as pltpu
from jax.sharding import PartitionSpec as P


def expert_forward(inputs, gate_weight, up_weight, down_weight):
    gate_sums = jnp.einsum("erd,edf->erf", inputs, gate_weight, preferred_element_type=jnp.float32)
    up_sums = jnp.einsum("erd,edf->erf", inputs, up_weight, preferred_element_type=jnp.float32)
    hidden = (jax.nn.silu(gate_sums) * up_sums).astype(jnp.bfloat16)
    expert_out = jnp.einsum(
        "erf,efd->erd", hidden, down_weight, preferred_element_type=jnp.float32
    ).astype(jnp.bfloat16)
    return ((gate_sums, up_sums, hidden), expert_out)


def expert_backward(inputs, out_grad, saved_state, gate_weight, up_weight, down_weight):
    gate_sums, up_sums, hidden = saved_state
    hidden_grad = jnp.einsum(
        "erd,efd->erf", out_grad, down_weight, preferred_element_type=jnp.float32
    )
    sigmoid = jax.nn.sigmoid(gate_sums)
    gate_back = (hidden_grad * up_sums * sigmoid * (1.0 + gate_sums * (1.0 - sigmoid))).astype(
        jnp.bfloat16
    )
    up_back = (hidden_grad * (gate_sums * sigmoid)).astype(jnp.bfloat16)
    slot_grad = jnp.einsum(
        "erf,edf->erd", gate_back, gate_weight, preferred_element_type=jnp.float32
    )
    slot_grad = (
        slot_grad
        + jnp.einsum("erf,edf->erd", up_back, up_weight, preferred_element_type=jnp.float32)
    ).astype(jnp.bfloat16)
    part_gate = jnp.einsum(
        "erd,erf->edf", inputs, gate_back, preferred_element_type=jnp.float32
    ).astype(jnp.bfloat16)
    part_up = jnp.einsum(
        "erd,erf->edf", inputs, up_back, preferred_element_type=jnp.float32
    ).astype(jnp.bfloat16)
    part_down = jnp.einsum(
        "erf,erd->efd", hidden, out_grad, preferred_element_type=jnp.float32
    ).astype(jnp.bfloat16)
    return (slot_grad, part_gate, part_up, part_down)


def shards(tokens, cotangent, expert_ids, gate_values, gate_weight, up_weight, down_weight):
    tok_rows, model_width = tokens.shape
    top_count = expert_ids.shape[1]
    exp_local = gate_weight.shape[0]
    peer_count = lax.axis_size("expert")
    experts = exp_local * peer_count
    slot_count = tok_rows * top_count
    capacity = (slot_count + slot_count // 12) // experts
    bf_zero = jnp.zeros((), jnp.bfloat16)
    flat_ids = expert_ids.reshape(slot_count)
    onehot = (flat_ids[:, None] == jnp.arange(experts, dtype=jnp.int32)[None, :]).astype(jnp.int32)
    slot_rank = jnp.sum((jnp.cumsum(onehot, axis=0) - 1) * onehot, axis=1)
    slot_dest = flat_ids * capacity + slot_rank
    slot_owner = (
        jnp.full((experts * capacity,), slot_count, jnp.int32)
        .at[slot_dest]
        .set(jnp.arange(slot_count, dtype=jnp.int32))
    )
    filled = slot_owner < slot_count
    owner_safe = jnp.where(filled, slot_owner, 0)
    source_row = owner_safe // top_count
    slot_gate = jnp.where(
        filled, jnp.take(gate_values.reshape(slot_count), owner_safe).astype(jnp.float32), 0.0
    )
    sent_tokens = jnp.where(filled[:, None], jnp.take(tokens, source_row, axis=0), bf_zero).reshape(
        experts, capacity, model_width
    )
    sent_grads = (
        slot_gate[:, None] * jnp.take(cotangent, source_row, axis=0).astype(jnp.float32)
    ).astype(jnp.bfloat16)
    sent_grads = sent_grads.reshape(experts, capacity, model_width)
    arrived = lax.all_to_all(sent_tokens, "expert", split_axis=0, concat_axis=1, tiled=True)
    saved_state, expert_out = expert_forward(arrived, gate_weight, up_weight, down_weight)
    returned = lax.all_to_all(expert_out, "expert", split_axis=1, concat_axis=0, tiled=True)
    arrived_grads = lax.all_to_all(sent_grads, "expert", split_axis=0, concat_axis=1, tiled=True)
    slot_grad, part_gate, part_up, part_down = expert_backward(
        arrived, arrived_grads, saved_state, gate_weight, up_weight, down_weight
    )
    returned_grads = lax.all_to_all(slot_grad, "expert", split_axis=1, concat_axis=0, tiled=True)

    def collect(returned_rows):
        picked = jnp.take(returned_rows.reshape(experts * capacity, model_width), slot_dest, axis=0)
        return picked.reshape(tok_rows, top_count, model_width).astype(jnp.float32)

    layer_out = jnp.sum(
        gate_values.astype(jnp.float32)[:, :, None] * collect(returned), axis=1
    ).astype(jnp.bfloat16)
    grad_tokens = jnp.sum(collect(returned_grads), axis=1).astype(jnp.bfloat16)
    grad_gate, grad_up, grad_down = (
        lax.psum_scatter(part_gate, "dp", scatter_dimension=1, tiled=True).astype(jnp.float32),
        lax.psum_scatter(part_up, "dp", scatter_dimension=1, tiled=True).astype(jnp.float32),
        lax.psum_scatter(part_down, "dp", scatter_dimension=1, tiled=True).astype(jnp.float32),
    )
    return (layer_out, grad_tokens, grad_gate, grad_up, grad_down)


def gathered_kernel(sizes, place_ref, tok_ref, cot_ref, wg_ref, wu_ref, wd_ref, out_ref, gtok_ref, gg_ref, gu_ref, gd_ref,
                    rank_s, gate_s, x_s, og_s, h_s, gb_s, ub_s, xs_s, hs_s, p_s, pg_s, out_acc, gtok_acc):
    peers, reps, rows, width, ff, exp_local, queue = sizes
    f32, bf16 = jnp.float32, jnp.bfloat16
    group = peers * rows
    expert = pl.program_id(0)
    own_rep = place_ref[1]
    expert_row = place_ref[0] * exp_local + expert
    dot = functools.partial(lax.dot_general, preferred_element_type=f32)
    nn, nt, tn = (((1,), (0,)), ((), ())), (((1,), (1,)), ((), ())), (((0,), (0,)), ((), ()))

    @pl.when(expert == 0)
    def _():
        out_acc[...] = jnp.zeros_like(out_acc)
        gtok_acc[...] = jnp.zeros_like(gtok_acc)
        before = lax.broadcasted_iota(jnp.int32, (group, group), 0)
        after = lax.broadcasted_iota(jnp.int32, (group, group), 1)
        triangle = jnp.where(before < after, 1.0, 0.0).astype(bf16)
        unit = jnp.where(before == after, 1.0, 0.0).astype(bf16)

        def tables(rep, carry):
            gates = tok_ref[:, rep, :, width:].reshape(group, tok_ref.shape[3] - width)
            chosen = jnp.where(gates.astype(f32) > 0.0, 1.0, 0.0).astype(bf16)
            gate_rows = dot(gates, unit, tn)
            rank_s[rep] = jnp.where(gate_rows > 0.0, dot(chosen, triangle, tn), -1.0)
            gate_s[rep] = gate_rows
            return carry

        lax.fori_loop(0, reps, tables, 0)

    def pick(rep, carry):
        rank = rank_s[rep, pl.ds(expert_row, 1), :]
        gate = gate_s[rep, pl.ds(expert_row, 1), :]
        match = lax.broadcasted_iota(jnp.int32, (queue, group), 0) == rank.astype(jnp.int32)
        choice = jnp.where(match, 1.0, 0.0).astype(bf16)
        gated = jnp.where(match, jnp.broadcast_to(gate, (queue, group)), 0.0).astype(bf16)
        at = pl.multiple_of(rep * queue, queue)
        x_s[pl.ds(at, queue), :] = dot(choice, tok_ref[:, rep, :, :width].reshape(group, width), nn).astype(bf16)
        og_s[pl.ds(at, queue), :] = dot(gated, cot_ref[:, rep].reshape(group, width), nn).astype(bf16)

        @pl.when(rep == own_rep)
        def _():
            p_s[...] = choice
            pg_s[...] = gated

        return carry

    lax.fori_loop(0, reps, pick, 0)

    tile = 256
    half = reps * queue // 2

    def middle(step, carry):
        col = pl.ds(pl.multiple_of(step // 2 * tile, tile), tile)
        row = pl.ds(pl.multiple_of(step % 2 * half, half), half)
        x = x_s[row, :]
        gate_sums = dot(x, wg_ref[0, :, col], nn)
        up_sums = dot(x, wu_ref[0, :, col], nn)
        hidden_grad = dot(og_s[row, :], wd_ref[0, col, :], nt)
        sigmoid = jax.nn.sigmoid(gate_sums)
        act = gate_sums * sigmoid
        h_s[row, col] = (act * up_sums).astype(bf16)
        gb_s[row, col] = (hidden_grad * up_sums * sigmoid * (1.0 + gate_sums * (1.0 - sigmoid))).astype(bf16)
        ub_s[row, col] = (hidden_grad * act).astype(bf16)
        return carry

    lax.fori_loop(0, ff // tile * 2, middle, 0)

    own = pl.ds(pl.multiple_of(own_rep * queue, queue), queue)

    def returns(step, carry):
        col = pl.ds(pl.multiple_of(step * tile, tile), tile)
        expert_out = dot(h_s[own, :], wd_ref[0, :, col], nn).astype(bf16)
        out_acc[:, col] += dot(pg_s[...], expert_out, tn)
        slot_grad = (dot(gb_s[own, :], wg_ref[0, col, :], nt) + dot(ub_s[own, :], wu_ref[0, col, :], nt)).astype(bf16)
        gtok_acc[:, col] += dot(p_s[...], slot_grad, tn)
        return carry

    lax.fori_loop(0, width // tile, returns, 0)

    wide, narrow = width // reps, ff // reps
    for rep in range(reps):
        @pl.when(own_rep == rep)
        def _():
            xs_s[...] = x_s[:, rep * wide:(rep + 1) * wide]
            hs_s[...] = h_s[:, rep * narrow:(rep + 1) * narrow]

    def sums(step, carry):
        col = pl.ds(pl.multiple_of(step * tile, tile), tile)
        gg_ref[0, :, col] = dot(xs_s[...], gb_s[:, col], tn)
        gu_ref[0, :, col] = dot(xs_s[...], ub_s[:, col], tn)
        return carry

    lax.fori_loop(0, ff // tile, sums, 0)

    def sums_down(step, carry):
        col = pl.ds(pl.multiple_of(step * tile, tile), tile)
        gd_ref[0, :, col] = dot(hs_s[...], og_s[:, col], tn)
        return carry

    lax.fori_loop(0, width // tile, sums_down, 0)

    @pl.when(expert == exp_local - 1)
    def _():
        out_ref[...] = out_acc[...].astype(bf16)
        gtok_ref[...] = gtok_acc[...].astype(bf16)


def gathered_shards(tokens, cotangent, expert_ids, gate_values, gate_weight, up_weight, down_weight):
    rows, width = tokens.shape
    top_count = expert_ids.shape[1]
    exp_local, _, ff = gate_weight.shape
    peers, reps = lax.axis_size("expert"), lax.axis_size("dp")
    experts = exp_local * peers
    slots = rows * top_count
    queue = (slots + slots // 12) // experts * peers
    f32, bf16 = jnp.float32, jnp.bfloat16
    lanes = 128
    chosen = expert_ids[:, :, None] == jnp.arange(lanes, dtype=jnp.int32)[None, None, :]
    gates = jnp.sum(jnp.where(chosen, gate_values[:, :, None].astype(f32), 0.0), axis=1).astype(bf16)
    packed = jnp.concatenate([tokens, gates], axis=1)
    tok_all = lax.all_gather(packed, ("expert", "dp"), axis=0, tiled=True).reshape(peers, reps, rows, width + lanes)
    cot_all = lax.all_gather(cotangent, ("expert", "dp"), axis=0, tiled=True).reshape(peers, reps, rows, width)
    place = jnp.stack([lax.axis_index("expert"), lax.axis_index("dp")]).astype(jnp.int32)
    sizes = (peers, reps, rows, width, ff, exp_local, queue)
    group, every = peers * rows, reps * queue
    whole = lambda shape: pl.BlockSpec(shape, lambda e, *_: (0,) * len(shape), pipeline_mode=pl.Buffered(1))
    each = lambda a, b: pl.BlockSpec((1, a, b), lambda e, *_: (e, 0, 0))
    out, gtok, gg, gu, gd = pl.pallas_call(
        functools.partial(gathered_kernel, sizes),
        grid_spec=pltpu.PrefetchScalarGridSpec(
            num_scalar_prefetch=1,
            grid=(exp_local,),
            in_specs=[whole(tok_all.shape), whole(cot_all.shape), each(width, ff), each(width, ff), each(ff, width)],
            out_specs=[whole((group, width)), whole((group, width)), each(width // reps, ff), each(width // reps, ff), each(ff // reps, width)],
            scratch_shapes=[
                pltpu.VMEM((reps, lanes, group), f32),
                pltpu.VMEM((reps, lanes, group), f32),
                pltpu.VMEM((every, width), bf16),
                pltpu.VMEM((every, width), bf16),
                pltpu.VMEM((every, ff), bf16),
                pltpu.VMEM((every, ff), bf16),
                pltpu.VMEM((every, ff), bf16),
                pltpu.VMEM((every, width // reps), bf16),
                pltpu.VMEM((every, ff // reps), bf16),
                pltpu.VMEM((queue, group), bf16),
                pltpu.VMEM((queue, group), bf16),
                pltpu.VMEM((group, width), f32),
                pltpu.VMEM((group, width), f32),
            ],
        ),
        out_shape=[
            jax.ShapeDtypeStruct((group, width), bf16),
            jax.ShapeDtypeStruct((group, width), bf16),
            jax.ShapeDtypeStruct((exp_local, width // reps, ff), f32),
            jax.ShapeDtypeStruct((exp_local, width // reps, ff), f32),
            jax.ShapeDtypeStruct((exp_local, ff // reps, width), f32),
        ],
        compiler_params=pltpu.CompilerParams(vmem_limit_bytes=60 * 1024 * 1024),
    )(place, tok_all, cot_all, gate_weight, up_weight, down_weight)
    layer_out = lax.psum_scatter(out, "expert", scatter_dimension=0, tiled=True)
    grad_tokens = lax.psum_scatter(gtok, "expert", scatter_dimension=0, tiled=True)
    return (layer_out, grad_tokens, gg, gu, gd)


def solution(mesh):
    blocks = mesh.shape["expert"] * mesh.shape["dp"]
    body = gathered_shards if blocks <= 16 else shards
    return jax.shard_map(
        body,
        mesh=mesh,
        in_specs=(
            P(("groups", "expert", "dp"), None),
            P(("groups", "expert", "dp"), None),
            P(("groups", "expert", "dp"), None),
            P(("groups", "expert", "dp"), None),
            P("expert", None, None),
            P("expert", None, None),
            P("expert", None, None),
        ),
        out_specs=(
            P(("groups", "expert", "dp"), None),
            P(("groups", "expert", "dp"), None),
            P(("groups", "expert"), "dp", None),
            P(("groups", "expert"), "dp", None),
            P(("groups", "expert"), "dp", None),
        ),
        check_vma=False,
    )
```

```python
import functools

import jax
import jax.numpy as jnp
from jax import lax
from jax.experimental import pallas as pl
from jax.experimental.pallas import tpu as pltpu
from jax.sharding import PartitionSpec as P


def expert_forward(inputs, gate_weight, up_weight, down_weight):
    gate_sums = jnp.einsum("erd,edf->erf", inputs, gate_weight, preferred_element_type=jnp.float32)
    up_sums = jnp.einsum("erd,edf->erf", inputs, up_weight, preferred_element_type=jnp.float32)
    hidden = (jax.nn.silu(gate_sums) * up_sums).astype(jnp.bfloat16)
    expert_out = jnp.einsum(
        "erf,efd->erd", hidden, down_weight, preferred_element_type=jnp.float32
    ).astype(jnp.bfloat16)
    return ((gate_sums, up_sums, hidden), expert_out)


def expert_backward(inputs, out_grad, saved_state, gate_weight, up_weight, down_weight):
    gate_sums, up_sums, hidden = saved_state
    hidden_grad = jnp.einsum(
        "erd,efd->erf", out_grad, down_weight, preferred_element_type=jnp.float32
    )
    sigmoid = jax.nn.sigmoid(gate_sums)
    gate_back = (hidden_grad * up_sums * sigmoid * (1.0 + gate_sums * (1.0 - sigmoid))).astype(
        jnp.bfloat16
    )
    up_back = (hidden_grad * (gate_sums * sigmoid)).astype(jnp.bfloat16)
    slot_grad = jnp.einsum(
        "erf,edf->erd", gate_back, gate_weight, preferred_element_type=jnp.float32
    )
    slot_grad = (
        slot_grad
        + jnp.einsum("erf,edf->erd", up_back, up_weight, preferred_element_type=jnp.float32)
    ).astype(jnp.bfloat16)
    part_gate = jnp.einsum(
        "erd,erf->edf", inputs, gate_back, preferred_element_type=jnp.float32
    ).astype(jnp.bfloat16)
    part_up = jnp.einsum(
        "erd,erf->edf", inputs, up_back, preferred_element_type=jnp.float32
    ).astype(jnp.bfloat16)
    part_down = jnp.einsum(
        "erf,erd->efd", hidden, out_grad, preferred_element_type=jnp.float32
    ).astype(jnp.bfloat16)
    return (slot_grad, part_gate, part_up, part_down)


def shards(tokens, cotangent, expert_ids, gate_values, gate_weight, up_weight, down_weight):
    tok_rows, model_width = tokens.shape
    top_count = expert_ids.shape[1]
    exp_local = gate_weight.shape[0]
    peer_count = lax.axis_size("expert")
    experts = exp_local * peer_count
    slot_count = tok_rows * top_count
    capacity = (slot_count + slot_count // 12) // experts
    bf_zero = jnp.zeros((), jnp.bfloat16)
    flat_ids = expert_ids.reshape(slot_count)
    onehot = (flat_ids[:, None] == jnp.arange(experts, dtype=jnp.int32)[None, :]).astype(jnp.int32)
    slot_rank = jnp.sum((jnp.cumsum(onehot, axis=0) - 1) * onehot, axis=1)
    slot_dest = flat_ids * capacity + slot_rank
    slot_owner = (
        jnp.full((experts * capacity,), slot_count, jnp.int32)
        .at[slot_dest]
        .set(jnp.arange(slot_count, dtype=jnp.int32))
    )
    filled = slot_owner < slot_count
    owner_safe = jnp.where(filled, slot_owner, 0)
    source_row = owner_safe // top_count
    slot_gate = jnp.where(
        filled, jnp.take(gate_values.reshape(slot_count), owner_safe).astype(jnp.float32), 0.0
    )
    sent_tokens = jnp.where(filled[:, None], jnp.take(tokens, source_row, axis=0), bf_zero).reshape(
        experts, capacity, model_width
    )
    sent_grads = (
        slot_gate[:, None] * jnp.take(cotangent, source_row, axis=0).astype(jnp.float32)
    ).astype(jnp.bfloat16)
    sent_grads = sent_grads.reshape(experts, capacity, model_width)
    arrived = lax.all_to_all(sent_tokens, "expert", split_axis=0, concat_axis=1, tiled=True)
    saved_state, expert_out = expert_forward(arrived, gate_weight, up_weight, down_weight)
    returned = lax.all_to_all(expert_out, "expert", split_axis=1, concat_axis=0, tiled=True)
    arrived_grads = lax.all_to_all(sent_grads, "expert", split_axis=0, concat_axis=1, tiled=True)
    slot_grad, part_gate, part_up, part_down = expert_backward(
        arrived, arrived_grads, saved_state, gate_weight, up_weight, down_weight
    )
    returned_grads = lax.all_to_all(slot_grad, "expert", split_axis=1, concat_axis=0, tiled=True)

    def collect(returned_rows):
        picked = jnp.take(returned_rows.reshape(experts * capacity, model_width), slot_dest, axis=0)
        return picked.reshape(tok_rows, top_count, model_width).astype(jnp.float32)

    layer_out = jnp.sum(
        gate_values.astype(jnp.float32)[:, :, None] * collect(returned), axis=1
    ).astype(jnp.bfloat16)
    grad_tokens = jnp.sum(collect(returned_grads), axis=1).astype(jnp.bfloat16)
    grad_gate, grad_up, grad_down = (
        lax.psum_scatter(part_gate, "dp", scatter_dimension=1, tiled=True).astype(jnp.float32),
        lax.psum_scatter(part_up, "dp", scatter_dimension=1, tiled=True).astype(jnp.float32),
        lax.psum_scatter(part_down, "dp", scatter_dimension=1, tiled=True).astype(jnp.float32),
    )
    return (layer_out, grad_tokens, grad_gate, grad_up, grad_down)


MESH = pl.DeviceIdType.MESH


def fused_kernel(sizes, tok_ref, cot_ref, wg_ref, wu_ref, wd_ref, out_ref, gtok_ref, gg_ref, gu_ref, gd_ref,
                 tok_s, cot_s, rank_s, gate_s, x_s, og_s, h_s, gb_s, ub_s, xs_s, hs_s, p_s, pg_s, out_acc, gtok_acc,
                 stage_s, land_s, send_sem, recv_sem, back_send, back_recv):
    peers, reps, rows, width, ff, exp_local, queue = sizes
    f32, bf16 = jnp.float32, jnp.bfloat16
    group = peers * rows
    phase, expert = pl.program_id(0), pl.program_id(1)
    me, rep_me = lax.axis_index("expert"), lax.axis_index("dp")
    core, side = rep_me % 2, rep_me // 2
    mate = side * 2 + (1 - core)
    across = (1 - side) * 2 + core
    across_mate = (1 - side) * 2 + (1 - core)
    expert_row = me * exp_local + expert
    dot = functools.partial(lax.dot_general, preferred_element_type=f32)
    nn, nt, tn = (((1,), (0,)), ((), ())), (((1,), (1,)), ((), ())), (((0,), (0,)), ((), ()))
    kept = (tok_s, cot_s)

    def push(what, where, rep, place, device, source=None):
        block = kept[what].at[where, rep]
        return pltpu.make_async_remote_copy(
            src_ref=block if source is None else source,
            dst_ref=block,
            send_sem=send_sem.at[what, place],
            recv_sem=recv_sem.at[what, where, rep],
            device_id=device,
            device_id_type=MESH,
        )

    def spread(what, where, offset, source=None):
        push(what, where, rep_me, peers - 1 + offset, {"dp": across}, source).start()
        push(what, where, rep_me, 2 * peers - 1 + offset, {"dp": mate}, source).start()

    def arrive(what, where, rep):
        push(what, where, rep, 0, {"dp": mate}).wait_recv()

    def back(which, offset):
        return pltpu.make_async_remote_copy(
            src_ref=stage_s.at[which, lax.rem(me + offset, peers)],
            dst_ref=land_s.at[which, me],
            send_sem=back_send.at[which, offset - 1],
            recv_sem=back_recv.at[which, me],
            device_id={"expert": lax.rem(me + offset, peers)},
            device_id_type=MESH,
        )

    @pl.when((phase == 0) & (expert == 0))
    def _():
        barrier = pltpu.get_barrier_semaphore()
        for offset in range(1, peers):
            pl.semaphore_signal(barrier, inc=1, device_id={"expert": lax.rem(me + offset, peers)}, device_id_type=MESH)
        for rep in (mate, across):
            pl.semaphore_signal(barrier, inc=1, device_id={"dp": rep}, device_id_type=MESH)
        pl.semaphore_wait(barrier, peers + 1)
        own = (tok_ref, cot_ref)
        for what in range(2):
            for offset in range(1, peers):
                push(what, me, rep_me, offset - 1, {"expert": lax.rem(me + offset, peers)}, own[what]).start()
            spread(what, me, 0, own[what])
        tok_s[me, rep_me] = tok_ref[...]
        cot_s[me, rep_me] = cot_ref[...]
        out_acc[...] = jnp.zeros_like(out_acc)
        gtok_acc[...] = jnp.zeros_like(gtok_acc)
        for what in range(2):
            for offset in range(1, peers):
                where = lax.rem(me + peers - offset, peers)
                arrive(what, where, rep_me)
                spread(what, where, offset)
        for what in range(2):
            for offset in range(peers):
                arrive(what, lax.rem(me + peers - offset, peers), mate)

    @pl.when((phase == 0) & (expert == 1))
    def _():
        for what in range(2):
            for offset in range(peers):
                where = lax.rem(me + peers - offset, peers)
                arrive(what, where, across)
                push(what, where, across, 3 * peers - 1 + offset, {"dp": mate}).start()

    @pl.when((phase == 1) & (expert == 0))
    def _():
        for what in range(2):
            for offset in range(peers):
                arrive(what, lax.rem(me + peers - offset, peers), across_mate)

    first = (side + phase) % 2 * 2

    @pl.when(expert == 0)
    def _():
        before = lax.broadcasted_iota(jnp.int32, (group, group), 0)
        after = lax.broadcasted_iota(jnp.int32, (group, group), 1)
        triangle = jnp.where(before < after, 1.0, 0.0).astype(bf16)
        unit = jnp.where(before == after, 1.0, 0.0).astype(bf16)

        def tables(at, carry):
            gates = tok_s[:, first + at, :, width:].reshape(group, tok_s.shape[3] - width)
            chosen = jnp.where(gates.astype(f32) > 0.0, 1.0, 0.0).astype(bf16)
            gate_rows = dot(gates, unit, tn)
            rank_s[at] = jnp.where(gate_rows > 0.0, dot(chosen, triangle, tn), -1.0)
            gate_s[at] = gate_rows
            return carry

        lax.fori_loop(0, 2, tables, 0)

    def pick(at, carry):
        rank = rank_s[at, pl.ds(expert_row, 1), :]
        gate = gate_s[at, pl.ds(expert_row, 1), :]
        match = lax.broadcasted_iota(jnp.int32, (queue, group), 0).astype(f32) == rank
        choice = jnp.where(match, 1.0, 0.0).astype(bf16)
        gated = jnp.where(match, jnp.broadcast_to(gate, (queue, group)), 0.0).astype(bf16)
        row = pl.ds(pl.multiple_of(at * queue, queue), queue)
        x_s[row, :] = dot(choice, tok_s[:, first + at, :, :width].reshape(group, width), nn).astype(bf16)
        og_s[row, :] = dot(gated, cot_s[:, first + at].reshape(group, width), nn).astype(bf16)

        @pl.when(at == core)
        def _():
            p_s[...] = choice
            pg_s[...] = gated

        return carry

    lax.fori_loop(0, 2, pick, 0)

    tile = 256

    def middle(step, carry):
        col = pl.ds(pl.multiple_of(step * tile, tile), tile)
        x = x_s[...]
        gate_sums = dot(x, wg_ref[0, :, col], nn)
        up_sums = dot(x, wu_ref[0, :, col], nn)
        hidden_grad = dot(og_s[...], wd_ref[0, col, :], nt)
        sigmoid = jax.nn.sigmoid(gate_sums)
        act = gate_sums * sigmoid
        h_s[:, col] = (act * up_sums).astype(bf16)
        gb_s[:, col] = (hidden_grad * up_sums * sigmoid * (1.0 + gate_sums * (1.0 - sigmoid))).astype(bf16)
        ub_s[:, col] = (hidden_grad * act).astype(bf16)
        return carry

    lax.fori_loop(0, ff // tile, middle, 0)

    @pl.when(phase == 0)
    def _():
        own = pl.ds(pl.multiple_of(core * queue, queue), queue)

        def returns(step, carry):
            col = pl.ds(pl.multiple_of(step * tile, tile), tile)
            expert_out = dot(h_s[own, :], wd_ref[0, :, col], nn).astype(bf16)
            out_acc[:, col] += dot(pg_s[...], expert_out, tn)
            slot_grad = (dot(gb_s[own, :], wg_ref[0, col, :], nt) + dot(ub_s[own, :], wu_ref[0, col, :], nt)).astype(bf16)
            gtok_acc[:, col] += dot(p_s[...], slot_grad, tn)
            return carry

        lax.fori_loop(0, width // tile, returns, 0)

    @pl.when((phase == 0) & (expert == exp_local - 1))
    def _():
        for which, acc in enumerate((out_acc, gtok_acc)):
            stage_s[which] = acc[...].astype(bf16).reshape(peers, rows, width)
            for offset in range(1, peers):
                back(which, offset).start()

    wide, narrow = width // reps, ff // reps
    for rep in range(reps):
        @pl.when(rep_me == rep)
        def _():
            xs_s[...] = x_s[:, rep * wide:(rep + 1) * wide]
            hs_s[...] = h_s[:, rep * narrow:(rep + 1) * narrow]

    @pl.when(phase == 0)
    def _():
        gg_ref[expert] = jnp.zeros((wide, ff), f32)
        gu_ref[expert] = jnp.zeros((wide, ff), f32)
        gd_ref[expert] = jnp.zeros((narrow, width), f32)

    def sums(step, carry):
        col = pl.ds(pl.multiple_of(step * tile, tile), tile)
        gg_ref[expert, :, col] += dot(xs_s[...], gb_s[:, col], tn)
        gu_ref[expert, :, col] += dot(xs_s[...], ub_s[:, col], tn)
        return carry

    lax.fori_loop(0, ff // tile, sums, 0)

    def sums_down(step, carry):
        col = pl.ds(pl.multiple_of(step * tile, tile), tile)
        gd_ref[expert, :, col] += dot(hs_s[...], og_s[:, col], tn)
        return carry

    lax.fori_loop(0, width // tile, sums_down, 0)

    @pl.when((phase == 1) & (expert == exp_local - 1))
    def _():
        for which, (acc, ref) in enumerate(((out_acc, out_ref), (gtok_acc, gtok_ref))):
            total = acc[pl.ds(pl.multiple_of(me * rows, rows), rows), :]
            for offset in range(1, peers):
                where = lax.rem(me + peers - offset, peers)
                pltpu.make_async_remote_copy(
                    src_ref=stage_s.at[which, 0],
                    dst_ref=land_s.at[which, where],
                    send_sem=back_send.at[which, 0],
                    recv_sem=back_recv.at[which, where],
                    device_id={"dp": mate},
                    device_id_type=MESH,
                ).wait_recv()
                total = total + land_s[which, where].astype(f32)
            ref[...] = total.astype(bf16)
        for which in range(2):
            for offset in range(1, peers):
                back(which, offset).wait_send()
            for place in range(4 * peers - 1):
                push(which, me, rep_me, place, {"dp": mate}).wait_send()


def fused_shards(tokens, cotangent, expert_ids, gate_values, gate_weight, up_weight, down_weight):
    rows, width = tokens.shape
    top_count = expert_ids.shape[1]
    exp_local, _, ff = gate_weight.shape
    peers, reps = lax.axis_size("expert"), lax.axis_size("dp")
    experts = exp_local * peers
    slots = rows * top_count
    queue = (slots + slots // 12) // experts * peers
    f32, bf16 = jnp.float32, jnp.bfloat16
    lanes = 128
    chosen = expert_ids[:, :, None] == jnp.arange(lanes, dtype=jnp.int32)[None, None, :]
    gates = jnp.sum(jnp.where(chosen, gate_values[:, :, None].astype(f32), 0.0), axis=1).astype(bf16)
    packed = jnp.concatenate([tokens, gates], axis=1)
    sizes = (peers, reps, rows, width, ff, exp_local, queue)
    group, every = peers * rows, 2 * queue
    wide, narrow = width // reps, ff // reps
    whole = lambda *shape: pl.BlockSpec(shape, lambda p, e: (0,) * len(shape), pipeline_mode=pl.Buffered(1))
    each = lambda a, b: pl.BlockSpec((1, a, b), lambda p, e: (e, 0, 0))
    return pl.pallas_call(
        functools.partial(fused_kernel, sizes),
        grid=(2, exp_local),
        in_specs=[whole(rows, width + lanes), whole(rows, width), each(width, ff), each(width, ff), each(ff, width)],
        out_specs=[whole(rows, width), whole(rows, width), whole(exp_local, wide, ff), whole(exp_local, wide, ff), whole(exp_local, narrow, width)],
        scratch_shapes=[
            pltpu.VMEM((peers, reps, rows, width + lanes), bf16),
            pltpu.VMEM((peers, reps, rows, width), bf16),
            pltpu.VMEM((2, lanes, group), f32),
            pltpu.VMEM((2, lanes, group), f32),
            pltpu.VMEM((every, width), bf16),
            pltpu.VMEM((every, width), bf16),
            pltpu.VMEM((every, ff), bf16),
            pltpu.VMEM((every, ff), bf16),
            pltpu.VMEM((every, ff), bf16),
            pltpu.VMEM((every, wide), bf16),
            pltpu.VMEM((every, narrow), bf16),
            pltpu.VMEM((queue, group), bf16),
            pltpu.VMEM((queue, group), bf16),
            pltpu.VMEM((group, width), f32),
            pltpu.VMEM((group, width), f32),
            pltpu.VMEM((2, peers, rows, width), bf16),
            pltpu.VMEM((2, peers, rows, width), bf16),
            pltpu.SemaphoreType.DMA((2, 4 * peers - 1)),
            pltpu.SemaphoreType.DMA((2, peers, reps)),
            pltpu.SemaphoreType.DMA((2, peers - 1)),
            pltpu.SemaphoreType.DMA((2, peers)),
        ],
        out_shape=[
            jax.ShapeDtypeStruct((rows, width), bf16),
            jax.ShapeDtypeStruct((rows, width), bf16),
            jax.ShapeDtypeStruct((exp_local, wide, ff), f32),
            jax.ShapeDtypeStruct((exp_local, wide, ff), f32),
            jax.ShapeDtypeStruct((exp_local, narrow, width), f32),
        ],
        compiler_params=pltpu.CompilerParams(vmem_limit_bytes=60 * 1024 * 1024, collective_id=0, has_side_effects=True),
    )(packed, cotangent, gate_weight, up_weight, down_weight)


def solution(mesh):
    fits = mesh.shape["expert"] <= 4 and mesh.shape["dp"] == 4
    body = fused_shards if fits else shards
    return jax.shard_map(
        body,
        mesh=mesh,
        in_specs=(
            P(("groups", "expert", "dp"), None),
            P(("groups", "expert", "dp"), None),
            P(("groups", "expert", "dp"), None),
            P(("groups", "expert", "dp"), None),
            P("expert", None, None),
            P("expert", None, None),
            P("expert", None, None),
        ),
        out_specs=(
            P(("groups", "expert", "dp"), None),
            P(("groups", "expert", "dp"), None),
            P(("groups", "expert"), "dp", None),
            P(("groups", "expert"), "dp", None),
            P(("groups", "expert"), "dp", None),
        ),
        check_vma=False,
    )
```

```python
import functools

import jax
import jax.numpy as jnp
from jax import lax
from jax.experimental import pallas as pl
from jax.experimental.pallas import tpu as pltpu
from jax.sharding import PartitionSpec as P


def expert_forward(inputs, gate_weight, up_weight, down_weight):
    gate_sums = jnp.einsum("erd,edf->erf", inputs, gate_weight, preferred_element_type=jnp.float32)
    up_sums = jnp.einsum("erd,edf->erf", inputs, up_weight, preferred_element_type=jnp.float32)
    hidden = (jax.nn.silu(gate_sums) * up_sums).astype(jnp.bfloat16)
    expert_out = jnp.einsum(
        "erf,efd->erd", hidden, down_weight, preferred_element_type=jnp.float32
    ).astype(jnp.bfloat16)
    return ((gate_sums, up_sums, hidden), expert_out)


def expert_backward(inputs, out_grad, saved_state, gate_weight, up_weight, down_weight):
    gate_sums, up_sums, hidden = saved_state
    hidden_grad = jnp.einsum(
        "erd,efd->erf", out_grad, down_weight, preferred_element_type=jnp.float32
    )
    sigmoid = jax.nn.sigmoid(gate_sums)
    gate_back = (hidden_grad * up_sums * sigmoid * (1.0 + gate_sums * (1.0 - sigmoid))).astype(
        jnp.bfloat16
    )
    up_back = (hidden_grad * (gate_sums * sigmoid)).astype(jnp.bfloat16)
    slot_grad = jnp.einsum(
        "erf,edf->erd", gate_back, gate_weight, preferred_element_type=jnp.float32
    )
    slot_grad = (
        slot_grad
        + jnp.einsum("erf,edf->erd", up_back, up_weight, preferred_element_type=jnp.float32)
    ).astype(jnp.bfloat16)
    part_gate = jnp.einsum(
        "erd,erf->edf", inputs, gate_back, preferred_element_type=jnp.float32
    ).astype(jnp.bfloat16)
    part_up = jnp.einsum(
        "erd,erf->edf", inputs, up_back, preferred_element_type=jnp.float32
    ).astype(jnp.bfloat16)
    part_down = jnp.einsum(
        "erf,erd->efd", hidden, out_grad, preferred_element_type=jnp.float32
    ).astype(jnp.bfloat16)
    return (slot_grad, part_gate, part_up, part_down)


def shards(tokens, cotangent, expert_ids, gate_values, gate_weight, up_weight, down_weight):
    tok_rows, model_width = tokens.shape
    top_count = expert_ids.shape[1]
    exp_local = gate_weight.shape[0]
    peer_count = lax.axis_size("expert")
    experts = exp_local * peer_count
    slot_count = tok_rows * top_count
    capacity = (slot_count + slot_count // 12) // experts
    bf_zero = jnp.zeros((), jnp.bfloat16)
    flat_ids = expert_ids.reshape(slot_count)
    onehot = (flat_ids[:, None] == jnp.arange(experts, dtype=jnp.int32)[None, :]).astype(jnp.int32)
    slot_rank = jnp.sum((jnp.cumsum(onehot, axis=0) - 1) * onehot, axis=1)
    slot_dest = flat_ids * capacity + slot_rank
    slot_owner = (
        jnp.full((experts * capacity,), slot_count, jnp.int32)
        .at[slot_dest]
        .set(jnp.arange(slot_count, dtype=jnp.int32))
    )
    filled = slot_owner < slot_count
    owner_safe = jnp.where(filled, slot_owner, 0)
    source_row = owner_safe // top_count
    slot_gate = jnp.where(
        filled, jnp.take(gate_values.reshape(slot_count), owner_safe).astype(jnp.float32), 0.0
    )
    sent_tokens = jnp.where(filled[:, None], jnp.take(tokens, source_row, axis=0), bf_zero).reshape(
        experts, capacity, model_width
    )
    sent_grads = (
        slot_gate[:, None] * jnp.take(cotangent, source_row, axis=0).astype(jnp.float32)
    ).astype(jnp.bfloat16)
    sent_grads = sent_grads.reshape(experts, capacity, model_width)
    arrived = lax.all_to_all(sent_tokens, "expert", split_axis=0, concat_axis=1, tiled=True)
    saved_state, expert_out = expert_forward(arrived, gate_weight, up_weight, down_weight)
    returned = lax.all_to_all(expert_out, "expert", split_axis=1, concat_axis=0, tiled=True)
    arrived_grads = lax.all_to_all(sent_grads, "expert", split_axis=0, concat_axis=1, tiled=True)
    slot_grad, part_gate, part_up, part_down = expert_backward(
        arrived, arrived_grads, saved_state, gate_weight, up_weight, down_weight
    )
    returned_grads = lax.all_to_all(slot_grad, "expert", split_axis=1, concat_axis=0, tiled=True)

    def collect(returned_rows):
        picked = jnp.take(returned_rows.reshape(experts * capacity, model_width), slot_dest, axis=0)
        return picked.reshape(tok_rows, top_count, model_width).astype(jnp.float32)

    layer_out = jnp.sum(
        gate_values.astype(jnp.float32)[:, :, None] * collect(returned), axis=1
    ).astype(jnp.bfloat16)
    grad_tokens = jnp.sum(collect(returned_grads), axis=1).astype(jnp.bfloat16)
    grad_gate, grad_up, grad_down = (
        lax.psum_scatter(part_gate, "dp", scatter_dimension=1, tiled=True).astype(jnp.float32),
        lax.psum_scatter(part_up, "dp", scatter_dimension=1, tiled=True).astype(jnp.float32),
        lax.psum_scatter(part_down, "dp", scatter_dimension=1, tiled=True).astype(jnp.float32),
    )
    return (layer_out, grad_tokens, grad_gate, grad_up, grad_down)


MESH = pl.DeviceIdType.MESH


def fused_kernel(sizes, tok_ref, cot_ref, wg_ref, wu_ref, wd_ref, out_ref, gtok_ref, gg_ref, gu_ref, gd_ref,
                 tok_s, cot_s, rank_s, gate_s, x_s, og_s, h_s, gb_s, ub_s, xs_s, hs_s, p_s, pg_s, out_acc, gtok_acc,
                 stage_s, land_s, send_sem, recv_sem, back_send, back_recv):
    peers, reps, rows, width, ff, exp_local, queue = sizes
    f32, bf16 = jnp.float32, jnp.bfloat16
    group = peers * rows
    phase, expert = pl.program_id(0), pl.program_id(1)
    me, rep_me = lax.axis_index("expert"), lax.axis_index("dp")
    core, side = rep_me % 2, rep_me // 2
    mate = side * 2 + (1 - core)
    across = (1 - side) * 2 + core
    across_mate = (1 - side) * 2 + (1 - core)
    expert_row = me * exp_local + expert
    dot = functools.partial(lax.dot_general, preferred_element_type=f32)
    nn, nt, tn = (((1,), (0,)), ((), ())), (((1,), (1,)), ((), ())), (((0,), (0,)), ((), ()))
    kept = (tok_s, cot_s)

    def push(what, where, rep, place, device, source=None):
        block = kept[what].at[where, rep]
        return pltpu.make_async_remote_copy(
            src_ref=block if source is None else source,
            dst_ref=block,
            send_sem=send_sem.at[what, place],
            recv_sem=recv_sem.at[what, where, rep],
            device_id=device,
            device_id_type=MESH,
        )

    def spread(what, where, source=None):
        push(what, where, rep_me, 2 * peers - 2 + where, {"dp": across}, source).start()
        push(what, where, rep_me, 3 * peers - 2 + where, {"dp": mate}, source).start()

    def along(what, where, distance, step, source=None):
        place = distance if step > 0 else peers - 1 + distance
        return push(what, where, rep_me, place, {"expert": me + step}, source)

    def arrive(what, where, rep):
        push(what, where, rep, 0, {"dp": mate}).wait_recv()

    def back(which, offset):
        return pltpu.make_async_remote_copy(
            src_ref=stage_s.at[which, lax.rem(me + offset, peers)],
            dst_ref=land_s.at[which, me],
            send_sem=back_send.at[which, offset - 1],
            recv_sem=back_recv.at[which, me],
            device_id={"expert": lax.rem(me + offset, peers)},
            device_id_type=MESH,
        )

    @pl.when((phase == 0) & (expert == 0))
    def _():
        barrier = pltpu.get_barrier_semaphore()
        for offset in range(1, peers):
            pl.semaphore_signal(barrier, inc=1, device_id={"expert": lax.rem(me + offset, peers)}, device_id_type=MESH)
        for rep in (mate, across):
            pl.semaphore_signal(barrier, inc=1, device_id={"dp": rep}, device_id_type=MESH)
        pl.semaphore_wait(barrier, peers + 1)
        own = (tok_ref, cot_ref)
        for what in range(2):
            @pl.when(me < peers - 1)
            def _():
                along(what, me, 0, 1, own[what]).start()

            @pl.when(me > 0)
            def _():
                along(what, me, 0, -1, own[what]).start()

            spread(what, me, own[what])
        tok_s[me, rep_me] = tok_ref[...]
        cot_s[me, rep_me] = cot_ref[...]
        out_acc[...] = jnp.zeros_like(out_acc)
        gtok_acc[...] = jnp.zeros_like(gtok_acc)
        for distance in range(1, peers):
            for what in range(2):
                @pl.when(me >= distance)
                def _():
                    arrive(what, me - distance, rep_me)

                    @pl.when(me < peers - 1)
                    def _():
                        along(what, me - distance, distance, 1).start()

                    spread(what, me - distance)

                @pl.when(me + distance < peers)
                def _():
                    arrive(what, me + distance, rep_me)

                    @pl.when(me > 0)
                    def _():
                        along(what, me + distance, distance, -1).start()

                    spread(what, me + distance)

    def relay(what):
        for where in range(peers):
            arrive(what, where, across)
            push(what, where, across, 4 * peers - 2 + where, {"dp": mate}).start()

    @pl.when((phase == 0) & (expert == exp_local // 2))
    def _():
        relay(0)

    @pl.when((phase == 1) & (expert == 0))
    def _():
        for what in range(2):
            for where in range(peers):
                arrive(what, where, mate)
                arrive(what, where, across_mate)

    tile = 256
    wide, narrow = width // reps, ff // reps

    def work(count, shift):
        all_rows = pl.ds(0, count * queue)

        @pl.when(expert == 0)
        def _():
            before = lax.broadcasted_iota(jnp.int32, (group, group), 0)
            after = lax.broadcasted_iota(jnp.int32, (group, group), 1)
            triangle = jnp.where(before < after, 1.0, 0.0).astype(bf16)
            unit = jnp.where(before == after, 1.0, 0.0).astype(bf16)

            def tables(at, carry):
                gates = tok_s[:, lax.rem(rep_me + shift + at, reps), :, width:].reshape(group, tok_s.shape[3] - width)
                chosen = jnp.where(gates.astype(f32) > 0.0, 1.0, 0.0).astype(bf16)
                gate_rows = dot(gates, unit, tn)
                rank_s[at] = jnp.where(gate_rows > 0.0, dot(chosen, triangle, tn), -1.0)
                gate_s[at] = gate_rows
                return carry

            lax.fori_loop(0, count, tables, 0)

        def pick(at, carry):
            rep = lax.rem(rep_me + shift + at, reps)
            rank = rank_s[at, pl.ds(expert_row, 1), :]
            gate = gate_s[at, pl.ds(expert_row, 1), :]
            match = lax.broadcasted_iota(jnp.int32, (queue, group), 0).astype(f32) == rank
            choice = jnp.where(match, 1.0, 0.0).astype(bf16)
            gated = jnp.where(match, jnp.broadcast_to(gate, (queue, group)), 0.0).astype(bf16)
            row = pl.ds(pl.multiple_of(at * queue, queue), queue)
            x_s[row, :] = dot(choice, tok_s[:, rep, :, :width].reshape(group, width), nn).astype(bf16)
            og_s[row, :] = dot(gated, cot_s[:, rep].reshape(group, width), nn).astype(bf16)
            p_s[...] = choice
            pg_s[...] = gated
            return carry

        lax.fori_loop(0, count, pick, 0)

        def middle(step, carry):
            col = pl.ds(pl.multiple_of(step * tile, tile), tile)
            x = x_s[all_rows, :]
            gate_sums = dot(x, wg_ref[0, :, col], nn)
            up_sums = dot(x, wu_ref[0, :, col], nn)
            hidden_grad = dot(og_s[all_rows, :], wd_ref[0, col, :], nt)
            sigmoid = jax.nn.sigmoid(gate_sums)
            act = gate_sums * sigmoid
            h_s[all_rows, col] = (act * up_sums).astype(bf16)
            gb_s[all_rows, col] = (hidden_grad * up_sums * sigmoid * (1.0 + gate_sums * (1.0 - sigmoid))).astype(bf16)
            ub_s[all_rows, col] = (hidden_grad * act).astype(bf16)
            return carry

        lax.fori_loop(0, ff // tile, middle, 0)

    def total(count, fresh):
        all_rows = pl.ds(0, count * queue)
        for rep in range(reps):
            @pl.when(rep_me == rep)
            def _():
                xs_s[all_rows, :] = x_s[all_rows, rep * wide:(rep + 1) * wide]
                hs_s[all_rows, :] = h_s[all_rows, rep * narrow:(rep + 1) * narrow]

        def put(ref, col, value):
            ref[expert, :, col] = value if fresh else ref[expert, :, col] + value

        def sums(step, carry):
            col = pl.ds(pl.multiple_of(step * tile, tile), tile)
            put(gg_ref, col, dot(xs_s[all_rows, :], gb_s[all_rows, col], tn))
            put(gu_ref, col, dot(xs_s[all_rows, :], ub_s[all_rows, col], tn))
            return carry

        lax.fori_loop(0, ff // tile, sums, 0)

        def sums_down(step, carry):
            col = pl.ds(pl.multiple_of(step * tile, tile), tile)
            put(gd_ref, col, dot(hs_s[all_rows, :], og_s[all_rows, col], tn))
            return carry

        lax.fori_loop(0, width // tile, sums_down, 0)

    @pl.when(phase == 0)
    def _():
        work(1, 0)
        own = pl.ds(0, queue)

        def returns(step, carry):
            col = pl.ds(pl.multiple_of(step * tile, tile), tile)
            expert_out = dot(h_s[own, :], wd_ref[0, :, col], nn).astype(bf16)
            out_acc[:, col] += dot(pg_s[...], expert_out, tn)
            slot_grad = (dot(gb_s[own, :], wg_ref[0, col, :], nt) + dot(ub_s[own, :], wu_ref[0, col, :], nt)).astype(bf16)
            gtok_acc[:, col] += dot(p_s[...], slot_grad, tn)
            return carry

        lax.fori_loop(0, width // tile, returns, 0)

        @pl.when(expert == exp_local - 1)
        def _():
            for which, acc in enumerate((out_acc, gtok_acc)):
                stage_s[which] = acc[...].astype(bf16).reshape(peers, rows, width)
                for offset in range(1, peers):
                    back(which, offset).start()

        total(1, True)

        @pl.when(expert == exp_local - 1)
        def _():
            relay(1)

    @pl.when(phase == 1)
    def _():
        work(reps - 1, 1)
        total(reps - 1, False)

    @pl.when((phase == 1) & (expert == exp_local - 1))
    def _():
        for which, (acc, ref) in enumerate(((out_acc, out_ref), (gtok_acc, gtok_ref))):
            added = acc[pl.ds(pl.multiple_of(me * rows, rows), rows), :]
            for offset in range(1, peers):
                where = lax.rem(me + peers - offset, peers)
                pltpu.make_async_remote_copy(
                    src_ref=stage_s.at[which, 0],
                    dst_ref=land_s.at[which, where],
                    send_sem=back_send.at[which, 0],
                    recv_sem=back_recv.at[which, where],
                    device_id={"dp": mate},
                    device_id_type=MESH,
                ).wait_recv()
                added = added + land_s[which, where].astype(f32)
            ref[...] = added.astype(bf16)
        for which in range(2):
            for offset in range(1, peers):
                back(which, offset).wait_send()
            for distance in range(peers - 1):
                @pl.when((me >= distance) & (me < peers - 1))
                def _():
                    along(which, me, distance, 1).wait_send()

                @pl.when((me + distance < peers) & (me > 0))
                def _():
                    along(which, me, distance, -1).wait_send()
            for place in range(2 * peers - 2, 5 * peers - 2):
                push(which, me, rep_me, place, {"dp": mate}).wait_send()


def fused_shards(tokens, cotangent, expert_ids, gate_values, gate_weight, up_weight, down_weight):
    rows, width = tokens.shape
    top_count = expert_ids.shape[1]
    exp_local, _, ff = gate_weight.shape
    peers, reps = lax.axis_size("expert"), lax.axis_size("dp")
    experts = exp_local * peers
    slots = rows * top_count
    queue = (slots + slots // 12) // experts * peers
    f32, bf16 = jnp.float32, jnp.bfloat16
    lanes = 128
    chosen = expert_ids[:, :, None] == jnp.arange(lanes, dtype=jnp.int32)[None, None, :]
    gates = jnp.sum(jnp.where(chosen, gate_values[:, :, None].astype(f32), 0.0), axis=1).astype(bf16)
    packed = jnp.concatenate([tokens, gates], axis=1)
    sizes = (peers, reps, rows, width, ff, exp_local, queue)
    group, every = peers * rows, (reps - 1) * queue
    wide, narrow = width // reps, ff // reps
    whole = lambda *shape: pl.BlockSpec(shape, lambda p, e: (0,) * len(shape), pipeline_mode=pl.Buffered(1))
    each = lambda a, b: pl.BlockSpec((1, a, b), lambda p, e: (e, 0, 0))
    return pl.pallas_call(
        functools.partial(fused_kernel, sizes),
        grid=(2, exp_local),
        in_specs=[whole(rows, width + lanes), whole(rows, width), each(width, ff), each(width, ff), each(ff, width)],
        out_specs=[whole(rows, width), whole(rows, width), whole(exp_local, wide, ff), whole(exp_local, wide, ff), whole(exp_local, narrow, width)],
        scratch_shapes=[
            pltpu.VMEM((peers, reps, rows, width + lanes), bf16),
            pltpu.VMEM((peers, reps, rows, width), bf16),
            pltpu.VMEM((reps - 1, lanes, group), f32),
            pltpu.VMEM((reps - 1, lanes, group), f32),
            pltpu.VMEM((every, width), bf16),
            pltpu.VMEM((every, width), bf16),
            pltpu.VMEM((every, ff), bf16),
            pltpu.VMEM((every, ff), bf16),
            pltpu.VMEM((every, ff), bf16),
            pltpu.VMEM((every, wide), bf16),
            pltpu.VMEM((every, narrow), bf16),
            pltpu.VMEM((queue, group), bf16),
            pltpu.VMEM((queue, group), bf16),
            pltpu.VMEM((group, width), f32),
            pltpu.VMEM((group, width), f32),
            pltpu.VMEM((2, peers, rows, width), bf16),
            pltpu.VMEM((2, peers, rows, width), bf16),
            pltpu.SemaphoreType.DMA((2, 5 * peers - 2)),
            pltpu.SemaphoreType.DMA((2, peers, reps)),
            pltpu.SemaphoreType.DMA((2, peers - 1)),
            pltpu.SemaphoreType.DMA((2, peers)),
        ],
        out_shape=[
            jax.ShapeDtypeStruct((rows, width), bf16),
            jax.ShapeDtypeStruct((rows, width), bf16),
            jax.ShapeDtypeStruct((exp_local, wide, ff), f32),
            jax.ShapeDtypeStruct((exp_local, wide, ff), f32),
            jax.ShapeDtypeStruct((exp_local, narrow, width), f32),
        ],
        compiler_params=pltpu.CompilerParams(vmem_limit_bytes=60 * 1024 * 1024, collective_id=0, has_side_effects=True),
    )(packed, cotangent, gate_weight, up_weight, down_weight)


def solution(mesh):
    fits = mesh.shape["expert"] <= 4 and mesh.shape["dp"] == 4
    body = fused_shards if fits else shards
    return jax.shard_map(
        body,
        mesh=mesh,
        in_specs=(
            P(("groups", "expert", "dp"), None),
            P(("groups", "expert", "dp"), None),
            P(("groups", "expert", "dp"), None),
            P(("groups", "expert", "dp"), None),
            P("expert", None, None),
            P("expert", None, None),
            P("expert", None, None),
        ),
        out_specs=(
            P(("groups", "expert", "dp"), None),
            P(("groups", "expert", "dp"), None),
            P(("groups", "expert"), "dp", None),
            P(("groups", "expert"), "dp", None),
            P(("groups", "expert"), "dp", None),
        ),
        check_vma=False,
    )
```

```python
import functools

import jax
import jax.numpy as jnp
from jax import lax
from jax.experimental import pallas as pl
from jax.experimental.pallas import tpu as pltpu
from jax.sharding import PartitionSpec as P


def expert_forward(inputs, gate_weight, up_weight, down_weight):
    gate_sums = jnp.einsum("erd,edf->erf", inputs, gate_weight, preferred_element_type=jnp.float32)
    up_sums = jnp.einsum("erd,edf->erf", inputs, up_weight, preferred_element_type=jnp.float32)
    hidden = (jax.nn.silu(gate_sums) * up_sums).astype(jnp.bfloat16)
    expert_out = jnp.einsum(
        "erf,efd->erd", hidden, down_weight, preferred_element_type=jnp.float32
    ).astype(jnp.bfloat16)
    return ((gate_sums, up_sums, hidden), expert_out)


def expert_backward(inputs, out_grad, saved_state, gate_weight, up_weight, down_weight):
    gate_sums, up_sums, hidden = saved_state
    hidden_grad = jnp.einsum(
        "erd,efd->erf", out_grad, down_weight, preferred_element_type=jnp.float32
    )
    sigmoid = jax.nn.sigmoid(gate_sums)
    gate_back = (hidden_grad * up_sums * sigmoid * (1.0 + gate_sums * (1.0 - sigmoid))).astype(
        jnp.bfloat16
    )
    up_back = (hidden_grad * (gate_sums * sigmoid)).astype(jnp.bfloat16)
    slot_grad = jnp.einsum(
        "erf,edf->erd", gate_back, gate_weight, preferred_element_type=jnp.float32
    )
    slot_grad = (
        slot_grad
        + jnp.einsum("erf,edf->erd", up_back, up_weight, preferred_element_type=jnp.float32)
    ).astype(jnp.bfloat16)
    part_gate = jnp.einsum(
        "erd,erf->edf", inputs, gate_back, preferred_element_type=jnp.float32
    ).astype(jnp.bfloat16)
    part_up = jnp.einsum(
        "erd,erf->edf", inputs, up_back, preferred_element_type=jnp.float32
    ).astype(jnp.bfloat16)
    part_down = jnp.einsum(
        "erf,erd->efd", hidden, out_grad, preferred_element_type=jnp.float32
    ).astype(jnp.bfloat16)
    return (slot_grad, part_gate, part_up, part_down)


def shards(tokens, cotangent, expert_ids, gate_values, gate_weight, up_weight, down_weight):
    tok_rows, model_width = tokens.shape
    top_count = expert_ids.shape[1]
    exp_local = gate_weight.shape[0]
    peer_count = lax.axis_size("expert")
    experts = exp_local * peer_count
    slot_count = tok_rows * top_count
    capacity = (slot_count + slot_count // 12) // experts
    bf_zero = jnp.zeros((), jnp.bfloat16)
    flat_ids = expert_ids.reshape(slot_count)
    onehot = (flat_ids[:, None] == jnp.arange(experts, dtype=jnp.int32)[None, :]).astype(jnp.int32)
    slot_rank = jnp.sum((jnp.cumsum(onehot, axis=0) - 1) * onehot, axis=1)
    slot_dest = flat_ids * capacity + slot_rank
    slot_owner = (
        jnp.full((experts * capacity,), slot_count, jnp.int32)
        .at[slot_dest]
        .set(jnp.arange(slot_count, dtype=jnp.int32))
    )
    filled = slot_owner < slot_count
    owner_safe = jnp.where(filled, slot_owner, 0)
    source_row = owner_safe // top_count
    slot_gate = jnp.where(
        filled, jnp.take(gate_values.reshape(slot_count), owner_safe).astype(jnp.float32), 0.0
    )
    sent_tokens = jnp.where(filled[:, None], jnp.take(tokens, source_row, axis=0), bf_zero).reshape(
        experts, capacity, model_width
    )
    sent_grads = (
        slot_gate[:, None] * jnp.take(cotangent, source_row, axis=0).astype(jnp.float32)
    ).astype(jnp.bfloat16)
    sent_grads = sent_grads.reshape(experts, capacity, model_width)
    arrived = lax.all_to_all(sent_tokens, "expert", split_axis=0, concat_axis=1, tiled=True)
    saved_state, expert_out = expert_forward(arrived, gate_weight, up_weight, down_weight)
    returned = lax.all_to_all(expert_out, "expert", split_axis=1, concat_axis=0, tiled=True)
    arrived_grads = lax.all_to_all(sent_grads, "expert", split_axis=0, concat_axis=1, tiled=True)
    slot_grad, part_gate, part_up, part_down = expert_backward(
        arrived, arrived_grads, saved_state, gate_weight, up_weight, down_weight
    )
    returned_grads = lax.all_to_all(slot_grad, "expert", split_axis=1, concat_axis=0, tiled=True)

    def collect(returned_rows):
        picked = jnp.take(returned_rows.reshape(experts * capacity, model_width), slot_dest, axis=0)
        return picked.reshape(tok_rows, top_count, model_width).astype(jnp.float32)

    layer_out = jnp.sum(
        gate_values.astype(jnp.float32)[:, :, None] * collect(returned), axis=1
    ).astype(jnp.bfloat16)
    grad_tokens = jnp.sum(collect(returned_grads), axis=1).astype(jnp.bfloat16)
    grad_gate, grad_up, grad_down = (
        lax.psum_scatter(part_gate, "dp", scatter_dimension=1, tiled=True).astype(jnp.float32),
        lax.psum_scatter(part_up, "dp", scatter_dimension=1, tiled=True).astype(jnp.float32),
        lax.psum_scatter(part_down, "dp", scatter_dimension=1, tiled=True).astype(jnp.float32),
    )
    return (layer_out, grad_tokens, grad_gate, grad_up, grad_down)


MESH = pl.DeviceIdType.MESH


def fused_kernel(sizes, tok_ref, cot_ref, wg_ref, wu_ref, wd_ref, out_ref, gtok_ref, gg_ref, gu_ref, gd_ref,
                 tok_s, cot_s, rank_s, gate_s, x_s, og_s, h_s, gb_s, ub_s, xs_s, hs_s, p_s, pg_s, out_acc, gtok_acc,
                 stage_s, land_s, send_sem, recv_sem, back_send, back_recv):
    peers, reps, rows, width, ff, exp_local, queue = sizes
    f32, bf16 = jnp.float32, jnp.bfloat16
    group = peers * rows
    phase, expert = pl.program_id(0), pl.program_id(1)
    me, rep_me = lax.axis_index("expert"), lax.axis_index("dp")
    core, side = rep_me % 2, rep_me // 2
    mate = side * 2 + (1 - core)
    across = (1 - side) * 2 + core
    across_mate = (1 - side) * 2 + (1 - core)
    expert_row = me * exp_local + expert
    dot = functools.partial(lax.dot_general, preferred_element_type=f32)
    nn, nt, tn = (((1,), (0,)), ((), ())), (((1,), (1,)), ((), ())), (((0,), (0,)), ((), ()))
    kept = (tok_s, cot_s)

    def push(what, where, rep, place, device, source=None):
        block = kept[what].at[where, rep]
        return pltpu.make_async_remote_copy(
            src_ref=block if source is None else source,
            dst_ref=block,
            send_sem=send_sem.at[what, place],
            recv_sem=recv_sem.at[what, where, rep],
            device_id=device,
            device_id_type=MESH,
        )

    def spread(what, where, source=None):
        push(what, where, rep_me, 2 * peers - 2 + where, {"dp": across}, source).start()
        push(what, where, rep_me, 3 * peers - 2 + where, {"dp": mate}, source).start()

    def along(what, where, distance, step, source=None):
        place = distance if step > 0 else peers - 1 + distance
        return push(what, where, rep_me, place, {"expert": me + step}, source)

    def arrive(what, where, rep):
        push(what, where, rep, 0, {"dp": mate}).wait_recv()

    def back(which, offset):
        return pltpu.make_async_remote_copy(
            src_ref=stage_s.at[which, lax.rem(me + offset, peers)],
            dst_ref=land_s.at[which, me],
            send_sem=back_send.at[which, offset - 1],
            recv_sem=back_recv.at[which, me],
            device_id={"expert": lax.rem(me + offset, peers)},
            device_id_type=MESH,
        )

    @pl.when((phase == 0) & (expert == 0))
    def _():
        barrier = pltpu.get_barrier_semaphore()
        for offset in range(1, peers):
            pl.semaphore_signal(barrier, inc=1, device_id={"expert": lax.rem(me + offset, peers)}, device_id_type=MESH)
        for rep in (mate, across):
            pl.semaphore_signal(barrier, inc=1, device_id={"dp": rep}, device_id_type=MESH)
        pl.semaphore_wait(barrier, peers + 1)
        own = (tok_ref, cot_ref)
        for what in range(2):
            @pl.when(me < peers - 1)
            def _():
                along(what, me, 0, 1, own[what]).start()

            @pl.when(me > 0)
            def _():
                along(what, me, 0, -1, own[what]).start()

            spread(what, me, own[what])
        tok_s[me, rep_me] = tok_ref[...]
        cot_s[me, rep_me] = cot_ref[...]
        out_acc[...] = jnp.zeros_like(out_acc)
        gtok_acc[...] = jnp.zeros_like(gtok_acc)
        for distance in range(1, peers):
            for what in range(2):
                @pl.when(me >= distance)
                def _():
                    arrive(what, me - distance, rep_me)

                    @pl.when(me < peers - 1)
                    def _():
                        along(what, me - distance, distance, 1).start()

                    spread(what, me - distance)

                @pl.when(me + distance < peers)
                def _():
                    arrive(what, me + distance, rep_me)

                    @pl.when(me > 0)
                    def _():
                        along(what, me + distance, distance, -1).start()

                    spread(what, me + distance)

    def relay(what):
        for where in range(peers):
            arrive(what, where, across)
            push(what, where, across, 4 * peers - 2 + where, {"dp": mate}).start()

    @pl.when((phase == 0) & (expert == exp_local // 2))
    def _():
        relay(0)

    @pl.when((phase == 1) & (expert == 0))
    def _():
        for what in range(2):
            for where in range(peers):
                arrive(what, where, mate)
                arrive(what, where, across_mate)

    tile = 256
    wide, narrow = width // reps, ff // reps

    def work(count, shift):
        all_rows = pl.ds(0, count * queue)

        @pl.when(expert == 0)
        def _():
            before = lax.broadcasted_iota(jnp.int32, (group, group), 0)
            after = lax.broadcasted_iota(jnp.int32, (group, group), 1)
            triangle = jnp.where(before < after, 1.0, 0.0).astype(bf16)
            unit = jnp.where(before == after, 1.0, 0.0).astype(bf16)

            def tables(at, carry):
                gates = tok_s[:, lax.rem(rep_me + shift + at, reps), :, width:].reshape(group, tok_s.shape[3] - width)
                chosen = jnp.where(gates.astype(f32) > 0.0, 1.0, 0.0).astype(bf16)
                gate_rows = dot(gates, unit, tn)
                rank_s[at] = jnp.where(gate_rows > 0.0, dot(chosen, triangle, tn), -1.0)
                gate_s[at] = gate_rows
                return carry

            lax.fori_loop(0, count, tables, 0)

        def pick(at, carry):
            rep = lax.rem(rep_me + shift + at, reps)
            rank = rank_s[at, pl.ds(expert_row, 1), :]
            gate = gate_s[at, pl.ds(expert_row, 1), :]
            match = lax.broadcasted_iota(jnp.int32, (queue, group), 0).astype(f32) == rank
            choice = jnp.where(match, 1.0, 0.0).astype(bf16)
            gated = jnp.where(match, jnp.broadcast_to(gate, (queue, group)), 0.0).astype(bf16)
            row = pl.ds(pl.multiple_of(at * queue, queue), queue)
            x_s[row, :] = dot(choice, tok_s[:, rep, :, :width].reshape(group, width), nn).astype(bf16)
            og_s[row, :] = dot(gated, cot_s[:, rep].reshape(group, width), nn).astype(bf16)
            p_s[...] = choice
            pg_s[...] = gated
            return carry

        lax.fori_loop(0, count, pick, 0)

        def middle(step, carry):
            col = pl.ds(pl.multiple_of(step * tile, tile), tile)
            x = x_s[all_rows, :]
            gate_sums = dot(x, wg_ref[0, :, col], nn)
            up_sums = dot(x, wu_ref[0, :, col], nn)
            hidden_grad = dot(og_s[all_rows, :], wd_ref[0, col, :], nt)
            sigmoid = jax.nn.sigmoid(gate_sums)
            act = gate_sums * sigmoid
            h_s[all_rows, col] = (act * up_sums).astype(bf16)
            gb_s[all_rows, col] = (hidden_grad * up_sums * sigmoid * (1.0 + gate_sums * (1.0 - sigmoid))).astype(bf16)
            ub_s[all_rows, col] = (hidden_grad * act).astype(bf16)
            return carry

        lax.fori_loop(0, ff // tile, middle, 0)

    def total(count, fresh):
        all_rows = pl.ds(0, count * queue)
        for rep in range(reps):
            @pl.when(rep_me == rep)
            def _():
                xs_s[all_rows, :] = x_s[all_rows, rep * wide:(rep + 1) * wide]
                hs_s[all_rows, :] = h_s[all_rows, rep * narrow:(rep + 1) * narrow]

        def put(ref, col, value):
            ref[expert, :, col] = value if fresh else ref[expert, :, col] + value

        def sums(step, carry):
            col = pl.ds(pl.multiple_of(step * tile, tile), tile)
            put(gg_ref, col, dot(xs_s[all_rows, :], gb_s[all_rows, col], tn))
            put(gu_ref, col, dot(xs_s[all_rows, :], ub_s[all_rows, col], tn))
            return carry

        lax.fori_loop(0, ff // tile, sums, 0)

        def sums_down(step, carry):
            col = pl.ds(pl.multiple_of(step * tile, tile), tile)
            put(gd_ref, col, dot(hs_s[all_rows, :], og_s[all_rows, col], tn))
            return carry

        lax.fori_loop(0, width // tile, sums_down, 0)

    @pl.when(phase == 0)
    def _():
        work(1, 0)
        own = pl.ds(0, queue)

        def returns(step, carry):
            col = pl.ds(pl.multiple_of(step * tile, tile), tile)
            expert_out = dot(h_s[own, :], wd_ref[0, :, col], nn).astype(bf16)
            out_acc[:, col] += dot(pg_s[...], expert_out, tn)
            return carry

        lax.fori_loop(0, width // tile, returns, 0)

        def send_back(which, acc):
            @pl.when(expert == exp_local - 1)
            def _():
                stage_s[which] = acc[...].astype(bf16).reshape(peers, rows, width)
                for offset in range(1, peers):
                    back(which, offset).start()

        send_back(0, out_acc)

        def returns_grad(step, carry):
            col = pl.ds(pl.multiple_of(step * tile, tile), tile)
            slot_grad = (dot(gb_s[own, :], wg_ref[0, col, :], nt) + dot(ub_s[own, :], wu_ref[0, col, :], nt)).astype(bf16)
            gtok_acc[:, col] += dot(p_s[...], slot_grad, tn)
            return carry

        lax.fori_loop(0, width // tile, returns_grad, 0)
        send_back(1, gtok_acc)

        total(1, True)

        @pl.when(expert == exp_local - 1)
        def _():
            relay(1)

    @pl.when(phase == 1)
    def _():
        work(reps - 1, 1)
        total(reps - 1, False)

    @pl.when((phase == 1) & (expert == exp_local - 1))
    def _():
        for which, (acc, ref) in enumerate(((out_acc, out_ref), (gtok_acc, gtok_ref))):
            added = acc[pl.ds(pl.multiple_of(me * rows, rows), rows), :]
            for offset in range(1, peers):
                where = lax.rem(me + peers - offset, peers)
                pltpu.make_async_remote_copy(
                    src_ref=stage_s.at[which, 0],
                    dst_ref=land_s.at[which, where],
                    send_sem=back_send.at[which, 0],
                    recv_sem=back_recv.at[which, where],
                    device_id={"dp": mate},
                    device_id_type=MESH,
                ).wait_recv()
                added = added + land_s[which, where].astype(f32)
            ref[...] = added.astype(bf16)
        for which in range(2):
            for offset in range(1, peers):
                back(which, offset).wait_send()
            for distance in range(peers - 1):
                @pl.when((me >= distance) & (me < peers - 1))
                def _():
                    along(which, me, distance, 1).wait_send()

                @pl.when((me + distance < peers) & (me > 0))
                def _():
                    along(which, me, distance, -1).wait_send()
            for place in range(2 * peers - 2, 5 * peers - 2):
                push(which, me, rep_me, place, {"dp": mate}).wait_send()


def fused_shards(tokens, cotangent, expert_ids, gate_values, gate_weight, up_weight, down_weight):
    rows, width = tokens.shape
    top_count = expert_ids.shape[1]
    exp_local, _, ff = gate_weight.shape
    peers, reps = lax.axis_size("expert"), lax.axis_size("dp")
    experts = exp_local * peers
    slots = rows * top_count
    queue = (slots + slots // 12) // experts * peers
    f32, bf16 = jnp.float32, jnp.bfloat16
    lanes = 128
    chosen = expert_ids[:, :, None] == jnp.arange(lanes, dtype=jnp.int32)[None, None, :]
    gates = jnp.sum(jnp.where(chosen, gate_values[:, :, None].astype(f32), 0.0), axis=1).astype(bf16)
    packed = jnp.concatenate([tokens, gates], axis=1)
    sizes = (peers, reps, rows, width, ff, exp_local, queue)
    group, every = peers * rows, (reps - 1) * queue
    wide, narrow = width // reps, ff // reps
    whole = lambda *shape: pl.BlockSpec(shape, lambda p, e: (0,) * len(shape), pipeline_mode=pl.Buffered(1))
    each = lambda a, b: pl.BlockSpec((1, a, b), lambda p, e: (e, 0, 0))
    return pl.pallas_call(
        functools.partial(fused_kernel, sizes),
        grid=(2, exp_local),
        in_specs=[whole(rows, width + lanes), whole(rows, width), each(width, ff), each(width, ff), each(ff, width)],
        out_specs=[whole(rows, width), whole(rows, width), whole(exp_local, wide, ff), whole(exp_local, wide, ff), whole(exp_local, narrow, width)],
        scratch_shapes=[
            pltpu.VMEM((peers, reps, rows, width + lanes), bf16),
            pltpu.VMEM((peers, reps, rows, width), bf16),
            pltpu.VMEM((reps - 1, lanes, group), f32),
            pltpu.VMEM((reps - 1, lanes, group), f32),
            pltpu.VMEM((every, width), bf16),
            pltpu.VMEM((every, width), bf16),
            pltpu.VMEM((every, ff), bf16),
            pltpu.VMEM((every, ff), bf16),
            pltpu.VMEM((every, ff), bf16),
            pltpu.VMEM((every, wide), bf16),
            pltpu.VMEM((every, narrow), bf16),
            pltpu.VMEM((queue, group), bf16),
            pltpu.VMEM((queue, group), bf16),
            pltpu.VMEM((group, width), f32),
            pltpu.VMEM((group, width), f32),
            pltpu.VMEM((2, peers, rows, width), bf16),
            pltpu.VMEM((2, peers, rows, width), bf16),
            pltpu.SemaphoreType.DMA((2, 5 * peers - 2)),
            pltpu.SemaphoreType.DMA((2, peers, reps)),
            pltpu.SemaphoreType.DMA((2, peers - 1)),
            pltpu.SemaphoreType.DMA((2, peers)),
        ],
        out_shape=[
            jax.ShapeDtypeStruct((rows, width), bf16),
            jax.ShapeDtypeStruct((rows, width), bf16),
            jax.ShapeDtypeStruct((exp_local, wide, ff), f32),
            jax.ShapeDtypeStruct((exp_local, wide, ff), f32),
            jax.ShapeDtypeStruct((exp_local, narrow, width), f32),
        ],
        compiler_params=pltpu.CompilerParams(vmem_limit_bytes=60 * 1024 * 1024, collective_id=0, has_side_effects=True),
    )(packed, cotangent, gate_weight, up_weight, down_weight)


def solution(mesh):
    fits = mesh.shape["expert"] <= 4 and mesh.shape["dp"] == 4
    body = fused_shards if fits else shards
    return jax.shard_map(
        body,
        mesh=mesh,
        in_specs=(
            P(("groups", "expert", "dp"), None),
            P(("groups", "expert", "dp"), None),
            P(("groups", "expert", "dp"), None),
            P(("groups", "expert", "dp"), None),
            P("expert", None, None),
            P("expert", None, None),
            P("expert", None, None),
        ),
        out_specs=(
            P(("groups", "expert", "dp"), None),
            P(("groups", "expert", "dp"), None),
            P(("groups", "expert"), "dp", None),
            P(("groups", "expert"), "dp", None),
            P(("groups", "expert"), "dp", None),
        ),
        check_vma=False,
    )
```
